32 devices in a mesh: gx: 2 (over core), gy: 4 (over y, x), gz: 4 (over z).
Axes of the slice: x: 2, y: 2, z: 4, core: 2. Of those that a mesh axis runs over, the one named last changes fastest.
Arguments:
- jacobian: bfloat16 [1024, 7, 135, 135], P(('gx', 'gy', 'gz')), may hold values from -6 to 6
- prolong: bfloat16 [1024, 135, 135], P(('gx', 'gy', 'gz')), may hold values from -0.5 to 0.5
- residual: bfloat16 [1024, 135], P(('gx', 'gy', 'gz')), may hold values from -6 to 6
- neighbours: int32 [1024, 6], P(('gx', 'gy', 'gz')), may hold values from -1 to 1023, as said below
- agg_map: int32 [1024], P(('gx', 'gy', 'gz')), may hold values from 0 to 127, as said below
- owners: int32 [128], P(('gx', 'gy', 'gz')), may hold values from 0 to 3, as said below
Outputs:
- coarse: bfloat16 [128, 7, 135, 135], P(('gx', 'gy', 'gz'))
- restricted: bfloat16 [128, 135], P(('gx', 'gy', 'gz'))
The draws below stay inside these ranges and needn't reach their ends.
Inputs may be any that keep to these rules, and one draw needn't show every extreme that they name: `neighbours`: elements form a structured grid of bricks of 4 x 4 x 2 per device, laid out by the device's gx, gy, gz index; inside a device their numbering is an arbitrary permutation. The neighbour in direction -x or +x lies on the same device or on the device one step along gx (likewise y with gy, z with gz); exactly 8, 8 and 16 elements of a device have their x, y and z neighbour of one side off the device or absent. `agg_map`: aggregates are cubes of 2 x 2 x 2 elements of one device's brick; device d holds aggregates d * 4 to (d + 1) * 4 - 1. `owners`: owners are multiples of 1; each device hands exactly 1 of its aggregates to each such owner.
All inputs are finite; a program needn't handle non-finite values.
Results may differ from the reference program's by a relative error of at most 0.0051.
Values may be sent and summed in bfloat16 or wider, within the bound.
A program may use at most 192 MiB of HBM per device.

```python
import jax
import jax.numpy as jnp
from jax import lax

B = 135
LX = 4
LY = 4
LZ = 2
E_DEV = 32
AGG_DEV = 4
SCAP = 1
ELEMS = 1024
CAPO = 4
N_GX = 2
N_GY = 4
N_GZ = 4


def cell_order(key):
    count = LX * LY * LZ
    devices = N_GX * N_GY * N_GZ
    keys = jax.random.split(jax.random.fold_in(key, 11), devices)
    return jax.vmap(lambda single: jax.random.permutation(single, count))(keys).astype(jnp.int32)


def cell_coords():
    count = LX * LY * LZ
    devices = N_GX * N_GY * N_GZ
    device = jnp.arange(devices, dtype=jnp.int32)[:, None]
    cell = jnp.arange(count, dtype=jnp.int32)[None, :]
    coord_x = device // (N_GY * N_GZ) * LX + cell // (LY * LZ)
    coord_y = device // N_GZ % N_GY * LY + cell // LZ % LY
    coord_z = device % N_GZ * LZ + cell % LZ
    return (coord_x, coord_y, coord_z)


def by_local(values, order):
    rows_index = jnp.arange(order.shape[0], dtype=jnp.int32)[:, None]
    return jnp.zeros(values.shape, jnp.int32).at[rows_index, order].set(values)


def draw_neighbours(key, part):
    count = LX * LY * LZ
    devices = N_GX * N_GY * N_GZ
    order = cell_order(key)
    coord_x, coord_y, coord_z = cell_coords()
    columns = []
    for step_x, step_y, step_z in ((-1, 0, 0), (1, 0, 0), (0, -1, 0), (0, 1, 0), (0, 0, -1), (0, 0, 1)):
        moved_x = coord_x + step_x
        moved_y = coord_y + step_y
        moved_z = coord_z + step_z
        inside = (moved_x >= 0) & (moved_x < LX * N_GX) & (moved_y >= 0) & (moved_y < LY * N_GY) & (moved_z >= 0) & (moved_z < LZ * N_GZ)
        moved_x = jnp.clip(moved_x, 0, LX * N_GX - 1)
        moved_y = jnp.clip(moved_y, 0, LY * N_GY - 1)
        moved_z = jnp.clip(moved_z, 0, LZ * N_GZ - 1)
        other_dev = (moved_x // LX * N_GY + moved_y // LY) * N_GZ + moved_z // LZ
        other_cell = (moved_x % LX * LY + moved_y % LY) * LZ + moved_z % LZ
        global_id = other_dev * count + order[other_dev, other_cell]
        columns.append(jnp.where(inside, global_id, -1))
    values = jnp.stack(columns, axis=-1).astype(jnp.int32)
    return by_local(values, order).reshape(devices * count, 6)


def draw_agg_map(key, part):
    count = LX * LY * LZ
    devices = N_GX * N_GY * N_GZ
    order = cell_order(key)
    coord_x, coord_y, coord_z = cell_coords()
    device = jnp.arange(devices, dtype=jnp.int32)[:, None]
    inner = (coord_x % LX // 2 * (LY // 2) + coord_y % LY // 2) * (LZ // 2) + coord_z % LZ // 2
    values = (device * (count // 8) + inner).astype(jnp.int32)
    return by_local(values, order).reshape(devices * count)


def draw_owners(key, part):
    devices = N_GX * N_GY * N_GZ
    keys = jax.random.split(jax.random.fold_in(key, 23), devices)
    listing = (jnp.arange(AGG_DEV, dtype=jnp.int32) // SCAP * (N_GZ // 4)).astype(jnp.int32)

    def single_device(single):
        return listing[jax.random.permutation(single, AGG_DEV)]
    return jax.vmap(single_device)(keys).reshape(-1).astype(jnp.int32)


def block_levels(key, shape, cuts, least, top_value):
    loudness, own = 1.0, jax.random.fold_in(key, 6)
    for dim, shards_of in cuts:
        draws = jnp.exp(jax.random.uniform(jax.random.fold_in(own, dim), (shards_of,), jnp.float32, least / len(cuts), top_value / len(cuts)))
        loudness = loudness * jnp.repeat(draws, shape[dim] // shards_of).reshape([-1 if axis == dim else 1 for axis in range(len(shape))])
    return loudness


def gaussian(key, shape, scale, reach, cuts=(), kind=jnp.bfloat16):
    array = scale * jax.random.normal(key, shape, jnp.float32)
    if cuts:
        array = array * block_levels(key, shape, cuts, -0.22, 0.18)
    return jnp.clip(array, -reach, reach).astype(kind)


def setup_inputs(seed: int = 0) -> dict:
    streams_of = jax.random.split(jax.random.key(seed), 7)
    return {
        "jacobian": gaussian(streams_of[0], (ELEMS, 7, B, B), 1.0, 6.0, ((0, 32),)),
        "prolong": gaussian(streams_of[1], (ELEMS, B, B), B ** -0.5, 0.5, ((0, 32),)),
        "residual": gaussian(streams_of[2], (ELEMS, B), 1.0, 6.0, ((0, 32),)),
        "neighbours": draw_neighbours(jax.random.fold_in(streams_of[6], 71), 0),
        "agg_map": draw_agg_map(jax.random.fold_in(streams_of[6], 71), 0),
        "owners": draw_owners(jax.random.fold_in(streams_of[6], 71), 0),
    }


def device_rows(device, jacobian, prolong, residual, neighbours, agg_map):
    first = (device * E_DEV).astype(jnp.int32)
    jac_dev = lax.dynamic_slice_in_dim(jacobian, first, E_DEV, 0)
    pro_dev = lax.dynamic_slice_in_dim(prolong, first, E_DEV, 0)
    res_dev = lax.dynamic_slice_in_dim(residual, first, E_DEV, 0)
    nbr_dev = lax.dynamic_slice_in_dim(neighbours, first, E_DEV, 0)
    agg_dev = lax.dynamic_slice_in_dim(agg_map, first, E_DEV, 0)
    is_valid = nbr_dev >= 0
    safe_ids = jnp.maximum(nbr_dev, 0)
    beside = jnp.where(is_valid[:, :, None, None], prolong[safe_ids], jnp.zeros((), jnp.bfloat16))
    gathered = jnp.concatenate([pro_dev[:, None], beside], axis=1)
    products = jnp.einsum("edij,edjk->edik", jac_dev.astype(jnp.float32), gathered.astype(jnp.float32)).astype(jnp.bfloat16)
    triple = jnp.einsum("eji,edjk->edik", pro_dev.astype(jnp.float32), products.astype(jnp.float32))
    same_agg = is_valid & (agg_map[safe_ids] == agg_dev[:, None])
    slot_ids = jnp.where(same_agg, 0, jnp.arange(1, 7, dtype=jnp.int32)[None, :])
    slot_ids = jnp.concatenate([jnp.zeros((E_DEV, 1), jnp.int32), slot_ids], axis=1)
    present = jnp.concatenate([jnp.ones((E_DEV, 1), bool), is_valid], axis=1)
    slot_hot = ((slot_ids[:, :, None] == jnp.arange(7, dtype=jnp.int32)) & present[:, :, None]).astype(jnp.float32)
    agg_hot = ((agg_dev - device * AGG_DEV)[:, None] == jnp.arange(AGG_DEV, dtype=jnp.int32)).astype(jnp.float32)
    coarse_rows = jnp.einsum("ea,eds,edik->asik", agg_hot, slot_hot, triple, precision=lax.Precision.HIGHEST)
    per_element = jnp.einsum("eji,ej->ei", pro_dev.astype(jnp.float32), res_dev.astype(jnp.float32))
    restr = jnp.dot(agg_hot.T, per_element, precision=lax.Precision.HIGHEST)
    return coarse_rows.astype(jnp.bfloat16), restr.astype(jnp.bfloat16)


def reference(jacobian, prolong, residual, neighbours, agg_map, owners):
    devices = N_GX * N_GY * N_GZ
    rows_all, restr_all = lax.map(lambda device: device_rows(device, jacobian, prolong, residual, neighbours, agg_map), jnp.arange(devices, dtype=jnp.int32))
    rows_all = rows_all.reshape(devices * AGG_DEV, 7, B, B)
    restr_all = restr_all.reshape(devices * AGG_DEV, B)
    owner_dev = owners.reshape(devices, AGG_DEV)
    counter = jnp.arange(AGG_DEV, dtype=jnp.int32)
    earlier = (owner_dev[:, None, :] == owner_dev[:, :, None]) & (counter[None, None, :] < counter[None, :, None])
    within = jnp.sum(earlier.astype(jnp.int32), axis=-1).reshape(-1)
    source = jnp.arange(devices * AGG_DEV, dtype=jnp.int32) // AGG_DEV
    target = (source // N_GZ) * N_GZ + owners
    row_ids = target * CAPO + (source % N_GZ) * SCAP + within
    coarse = jnp.zeros((devices * CAPO, 7, B, B), jnp.bfloat16).at[row_ids].set(rows_all)
    restricted = jnp.zeros((devices * CAPO, B), jnp.bfloat16).at[row_ids].set(restr_all)
    return coarse, restricted
```

```python
import jax
import jax.numpy as jnp
from jax import lax
from jax.experimental import pallas as pl
from jax.experimental.pallas import tpu as pltpu
from jax.sharding import PartitionSpec as P

LX = 4
LY = 4
LZ = 2


def from_behind(value, axis, steps):
    count = lax.axis_size(axis)
    initial, last = (max(0, -steps), min(count, count - steps))
    return lax.ppermute(value, axis, [(source, source + steps) for source in range(initial, last)])


def fetch_faces(blocks, axis_num, offset):
    if axis_num == 0:
        return from_behind(blocks, "gx", offset)
    if axis_num == 1:
        return from_behind(blocks, "gy", offset)
    return from_behind(blocks, "gz", offset)


def coarse_kernel(columns, slots, aggs, dest, prolong, faces, jacobian, out_slots, aggs_here):
    elems, width, _ = prolong.shape
    head = width // 128 * 128
    rest = width - head
    zero_block = elems + max(face.shape[0] for face in faces)
    step_rows = 5 if width % 5 == 0 else 1

    def kernel(col_ref, slot_ref, agg_ref, dest_ref, p_ref, *refs):
        face_refs = refs[:6]
        j_ref, head_ref, tail_ref, pool, flipped, near, far, total = refs[6:]
        k = pl.program_id(0)

        @pl.when(k == 0)
        def _():
            total[...] = jnp.zeros_like(total)
            head_ref[...] = jnp.zeros_like(head_ref)
            tail_ref[...] = jnp.zeros_like(tail_ref)
            pool[zero_block] = jnp.zeros((width, width), pool.dtype)

            @pl.loop(0, elems)
            def _(e):
                pool[e] = p_ref[e]
                flipped[e] = p_ref[e].astype(jnp.float32).T.astype(flipped.dtype)

        for d, face_ref in enumerate(face_refs):

            @pl.when(k == d + 1)
            def _(face_ref=face_ref):
                @pl.loop(0, face_ref.shape[0])
                def _(n):
                    pool[elems + n] = face_ref[n]

        @pl.loop(0, width // step_rows)
        def _(c):
            part = j_ref[0, pl.ds(c * step_rows, step_rows)].astype(jnp.float32)
            part = part.reshape(step_rows * elems, width)
            rows = pl.ds(pl.multiple_of(c * step_rows * elems, 8), step_rows * elems)
            near[rows, :] = part[:, :head]
            far[rows, :rest] = part[:, head:]

        @pl.loop(0, elems // 4)
        def _(group):
            for u in range(4):
                e = group * 4 + u
                own = jnp.concatenate(
                    [
                        near[pl.ds(e, width, stride=elems), :],
                        far[pl.ds(e, width, stride=elems), :],
                    ],
                    axis=1,
                )[:, :width].astype(jnp.bfloat16)
                product = jnp.dot(
                    own, pool[col_ref[e * 7 + k]], preferred_element_type=jnp.float32
                ).astype(jnp.bfloat16)
                triple = jnp.dot(flipped[e], product, preferred_element_type=jnp.float32)
                total[agg_ref[e], slot_ref[e * 7 + k]] += triple

        @pl.when(k == 6)
        def _():
            @pl.loop(0, aggs_here)
            def _(a):
                to = dest_ref[a]
                for s in range(7):
                    row = total[a, s]
                    head_ref[to, s] = row[:, :head].astype(jnp.bfloat16)
                    tail_ref[to, :, s * rest : (s + 1) * rest] = row[:, head:].astype(jnp.bfloat16)

    whole = pl.BlockSpec(memory_space=pltpu.VMEM)
    return pl.pallas_call(
        kernel,
        grid_spec=pltpu.PrefetchScalarGridSpec(
            num_scalar_prefetch=4,
            grid=(7,),
            in_specs=[whole] * 7
            + [pl.BlockSpec((1, width, elems, width), lambda k, *_: (k, 0, 0, 0))],
            out_specs=[whole, whole],
            scratch_shapes=[
                pltpu.VMEM((zero_block + 1, width, width), jnp.bfloat16),
                pltpu.VMEM((elems, width, width), jnp.bfloat16),
                pltpu.VMEM((width * elems, head), jnp.float32),
                pltpu.VMEM((width * elems, 128), jnp.float32),
                pltpu.VMEM((aggs_here, 7, width, width), jnp.float32),
            ],
        ),
        out_shape=[
            jax.ShapeDtypeStruct((out_slots, 7, width, head), jnp.bfloat16),
            jax.ShapeDtypeStruct((out_slots, width, pl.cdiv(7 * rest, 128) * 128), jnp.bfloat16),
        ],
        compiler_params=pltpu.CompilerParams(vmem_limit_bytes=56 << 20),
    )(columns, slots, aggs, dest, prolong, *faces, jnp.transpose(jacobian, (1, 2, 0, 3)))


def body(jacobian, prolong, residual, neighbours, agg_map, owners):
    elems = jacobian.shape[0]
    width = prolong.shape[1]
    aggs_here = owners.shape[0]
    size_y = lax.axis_size("gy")
    size_z = lax.axis_size("gz")
    per_owner = aggs_here // 4
    device = (lax.axis_index("gx") * size_y + lax.axis_index("gy")) * size_z + lax.axis_index("gz")
    id_base = device * elems
    local_ids = neighbours - id_base
    on_device = (local_ids >= 0) & (local_ids < elems)
    is_valid = neighbours >= 0
    off_device = is_valid & jnp.logical_not(on_device)
    zero_block = elems + max(LY * LZ, LX * LZ, LX * LY)
    strides = (size_y * size_z, size_z, 1)
    face_sizes = (LY * LZ, LX * LZ, LX * LY)
    flat_blocks = prolong.reshape(elems, width * width)
    elem_counter = jnp.arange(elems, dtype=jnp.int32)
    faces = []
    columns = [elem_counter]
    for direction in range(6):
        axis_num = direction // 2
        offset = 1 if direction % 2 == 0 else -1
        source_base = id_base - offset * strides[axis_num] * elems
        source_ids = neighbours[:, direction] - source_base
        face_count = face_sizes[axis_num]
        opposite = direction ^ 1
        on_face = jnp.logical_not(on_device[:, opposite])
        face_rank = jnp.cumsum(on_face.astype(jnp.int32)) - 1
        pack_select = (
            (jnp.arange(face_count, dtype=jnp.int32)[:, None] == face_rank[None, :])
            & on_face[None, :]
        ).astype(jnp.bfloat16)
        packed = jnp.dot(pack_select, flat_blocks, preferred_element_type=jnp.float32).astype(
            jnp.bfloat16
        )
        fetched = fetch_faces(packed, axis_num, offset)
        lower = off_device[None, :, direction] & (source_ids[None, :] < source_ids[:, None])
        position = jnp.sum(lower.astype(jnp.int32), axis=1)
        far_column = elems + position
        faces.append(fetched.reshape(face_count, width, width))
        near_column = jnp.where(on_device[:, direction], local_ids[:, direction], far_column)
        columns.append(jnp.where(is_valid[:, direction], near_column, zero_block))
    near_agg = agg_map[jnp.clip(local_ids, 0, elems - 1)]
    same_agg = on_device & (near_agg == agg_map[:, None])
    slot_ids = jnp.where(same_agg, 0, jnp.arange(1, 7, dtype=jnp.int32)[None, :])
    slot_ids = jnp.concatenate([jnp.zeros((elems, 1), jnp.int32), slot_ids], axis=1)
    agg_hot = (
        (agg_map - device * aggs_here)[:, None] == jnp.arange(aggs_here, dtype=jnp.int32)
    ).astype(jnp.float32)
    per_element = jnp.einsum("eji,ej->ei", prolong, residual, preferred_element_type=jnp.float32)
    restr = jnp.dot(agg_hot.T, per_element, precision=lax.Precision.HIGHEST).astype(jnp.bfloat16)
    agg_counter = jnp.arange(aggs_here, dtype=jnp.int32)
    earlier = (owners[None, :] == owners[:, None]) & (agg_counter[None, :] < agg_counter[:, None])
    within = jnp.sum(earlier.astype(jnp.int32), axis=1)
    send_slot = owners * per_owner + within
    select = (
        jnp.arange(size_z * per_owner, dtype=jnp.int32)[:, None] == send_slot[None, :]
    ).astype(jnp.bfloat16)
    heads, tails = coarse_kernel(
        jnp.stack(columns, axis=1).reshape(-1),
        slot_ids.reshape(-1),
        agg_map - device * aggs_here,
        send_slot,
        prolong,
        faces,
        jacobian,
        size_z * per_owner,
        aggs_here,
    )
    send_restr = jnp.dot(select, restr, preferred_element_type=jnp.float32).astype(jnp.bfloat16)
    heads = lax.all_to_all(heads, "gz", split_axis=0, concat_axis=0, tiled=True)
    tails = lax.all_to_all(tails, "gz", split_axis=0, concat_axis=0, tiled=True)
    restricted = lax.all_to_all(send_restr, "gz", split_axis=0, concat_axis=0, tiled=True)
    rest = width - heads.shape[3]
    tails = tails[:, :, : 7 * rest].reshape(-1, width, 7, rest).transpose(0, 2, 1, 3)
    return (jnp.concatenate([heads, tails], axis=3), restricted)


def solution(mesh):
    return jax.shard_map(
        body,
        mesh=mesh,
        in_specs=(
            P(("gx", "gy", "gz"), None, None, None),
            P(("gx", "gy", "gz"), None, None),
            P(("gx", "gy", "gz"), None),
            P(("gx", "gy", "gz"), None),
            P(("gx", "gy", "gz")),
            P(("gx", "gy", "gz")),
        ),
        out_specs=(P(("gx", "gy", "gz"), None, None, None), P(("gx", "gy", "gz"), None)),
        check_vma=False,
    )
```

```python
import jax
import jax.numpy as jnp
from jax import lax
from jax.experimental import pallas as pl
from jax.experimental.pallas import tpu as pltpu
from jax.sharding import PartitionSpec as P


LX = 4
LY = 4
LZ = 2
LANES = 128
UNROLL = 4


def from_behind(value, axis, steps):
    count = lax.axis_size(axis)
    initial, last = (max(0, -steps), min(count, count - steps))
    return lax.ppermute(value, axis, [(source, source + steps) for source in range(initial, last)])


def whole():
    return pl.BlockSpec(memory_space=pltpu.VMEM)


def params():
    return pltpu.CompilerParams(vmem_limit_bytes=56 << 20)


def cost(pairs, width):
    return pl.CostEstimate(
        flops=pairs * 96 * width * width * width,
        bytes_accessed=pairs * 4 * width * width,
        transcendentals=0,
    )


def pack_kernel(picks, prolong, counts):
    _, width, _ = prolong.shape
    rest = width - LANES

    def kernel(pick_ref, p_ref, *outs):
        for d, (out, count) in enumerate(zip(outs, counts)):
            for n in range(count):
                block = p_ref[pick_ref[d, n]]
                out[n] = block[:, :LANES]
                out[count, :, n * rest : (n + 1) * rest] = block[:, LANES:]

    return pl.pallas_call(
        kernel,
        grid_spec=pltpu.PrefetchScalarGridSpec(
            num_scalar_prefetch=1,
            grid=(1,),
            in_specs=[whole()],
            out_specs=[whole()] * len(counts),
        ),
        out_shape=[jax.ShapeDtypeStruct((n + 1, width, LANES), prolong.dtype) for n in counts],
        compiler_params=params(),
    )(picks, prolong)


def spread(j_ref, near, far):
    _, width, elems, _ = j_ref.shape
    step_rows = 5 if width % 5 == 0 else 1
    rest = width - LANES

    @pl.loop(0, width // step_rows)
    def _(c):
        part = j_ref[0, pl.ds(c * step_rows, step_rows)].astype(jnp.float32)
        part = part.reshape(step_rows * elems, width)
        rows = pl.ds(pl.multiple_of(c * step_rows * elems, 8), step_rows * elems)
        near[rows, :] = part[:, :LANES]
        far[rows, :rest] = part[:, LANES:]


def own_block(near, far, e, width, elems):
    rows = pl.ds(e, width, stride=elems)
    both = jnp.concatenate([near[rows, :], far[rows, :]], axis=1)
    return both[:, :width].astype(jnp.bfloat16)


def mul(a, b):
    return jnp.dot(a, b, preferred_element_type=jnp.float32)


def spread_scratch(width, elems):
    return [pltpu.VMEM((width * elems, LANES), jnp.float32)] * 2


def jac_spec(width, elems, first):
    return pl.BlockSpec((1, width, elems, width), lambda k, *_: (first + k, 0, 0, 0))


def own_kernel(table, prolong, jac, aggs_here):
    elems, width, _ = prolong.shape

    def kernel(table_ref, p_ref, j_ref, total, flipped, near, far):
        total[...] = jnp.zeros_like(total)
        spread(j_ref, near, far)

        @pl.loop(0, elems // UNROLL)
        def _(group):
            at = [group * UNROLL + u for u in range(UNROLL)]
            products = [
                mul(own_block(near, far, e, width, elems), p_ref[e]).astype(jnp.bfloat16)
                for e in at
            ]
            turned = [p_ref[e].astype(jnp.float32).T.astype(flipped.dtype) for e in at]
            triples = [mul(t, product) for t, product in zip(turned, products)]
            for e, t, triple in zip(at, turned, triples):
                flipped[e] = t
                total[table_ref[7, e]] += triple

    return pl.pallas_call(
        kernel,
        grid_spec=pltpu.PrefetchScalarGridSpec(
            num_scalar_prefetch=1,
            grid=(1,),
            in_specs=[whole(), jac_spec(width, elems, 0)],
            out_specs=[whole(), whole()],
            scratch_shapes=spread_scratch(width, elems),
        ),
        out_shape=[
            jax.ShapeDtypeStruct((aggs_here, width, width), jnp.float32),
            jax.ShapeDtypeStruct(prolong.shape, prolong.dtype),
        ],
        cost_estimate=cost(elems, width),
        compiler_params=params(),
    )(table, prolong, jac)


def side_kernel(table, dest, prolong, flipped, carry, faces, jac, first, out_slots, restr=None):
    elems, width, _ = prolong.shape
    aggs_here = carry.shape[0]
    rest = width - LANES
    count = len(faces)
    zero_block = elems + max(face.shape[0] for face in faces) - 1
    final = restr is not None
    emitted = range(0 if final else 1, count + 1)
    rows_out = len(emitted)

    def kernel(table_ref, dest_ref, p_ref, t_ref, carry_ref, *refs):
        face_refs, refs = refs[:count], refs[count:]
        if final:
            restr_ref, refs = refs[0], refs[1:]
        j_ref, out, refs = refs[0], refs[1], refs[2:]
        if not final:
            next_ref, refs = refs[0], refs[1:]
        pool, near, far, total = refs
        k = pl.program_id(0)

        @pl.when(k == 0)
        def _():
            out[...] = jnp.zeros_like(out)
            total[...] = jnp.zeros_like(total)
            pool[zero_block] = jnp.zeros((width, width), pool.dtype)

            @pl.loop(0, aggs_here)
            def _(a):
                total[a, 0] = carry_ref[a]

            @pl.loop(0, elems)
            def _(e):
                pool[e] = p_ref[e]

        for d, face_ref in enumerate(face_refs):

            @pl.when(k == d)
            def _(face_ref=face_ref):
                last = face_ref.shape[0] - 1
                for n in range(last):
                    pool[elems + n, :, :LANES] = face_ref[n]
                    pool[elems + n, :, LANES:] = face_ref[last, :, n * rest : (n + 1) * rest]

        spread(j_ref, near, far)

        @pl.loop(0, elems // UNROLL)
        def _(group):
            at = [group * UNROLL + u for u in range(UNROLL)]
            codes = [table_ref[first + k, e] for e in at]
            products = [
                mul(own_block(near, far, e, width, elems), pool[code // 2]).astype(jnp.bfloat16)
                for e, code in zip(at, codes)
            ]
            triples = [mul(t_ref[e], product) for e, product in zip(at, products)]
            for e, code, triple in zip(at, codes, triples):
                total[table_ref[7, e], jnp.where(code % 2 == 1, 0, k + 1)] += triple

        @pl.when(k == count - 1)
        def _():
            for a in range(aggs_here):
                to = dest_ref[a]
                for i, s in enumerate(emitted):
                    row = total[a, s].astype(jnp.bfloat16)
                    out[to, i] = row[:, :LANES]
                    out[to, rows_out, :, i * rest : (i + 1) * rest] = row[:, LANES:]
                if final:
                    lane = rows_out * rest
                    out[to, rows_out, :, lane : lane + 1] = restr_ref[:, a : a + 1]
                else:
                    next_ref[a] = total[a, 0]

    out_shape = [jax.ShapeDtypeStruct((out_slots, rows_out + 1, width, LANES), jnp.bfloat16)]
    if not final:
        out_shape.append(jax.ShapeDtypeStruct(carry.shape, carry.dtype))
    inputs = [prolong, flipped, carry, *faces] + ([restr] if final else [])
    return pl.pallas_call(
        kernel,
        grid_spec=pltpu.PrefetchScalarGridSpec(
            num_scalar_prefetch=2,
            grid=(count,),
            in_specs=[whole()] * len(inputs) + [jac_spec(width, elems, first)],
            out_specs=[whole()] * len(out_shape),
            scratch_shapes=[pltpu.VMEM((zero_block + 1, width, width), jnp.bfloat16)]
            + spread_scratch(width, elems)
            + [pltpu.VMEM((aggs_here, count + 1, width, width), jnp.float32)],
        ),
        out_shape=out_shape,
        cost_estimate=cost(elems * count, width),
        compiler_params=params(),
    )(table, dest, *inputs, jac)


def body(jacobian, prolong, residual, neighbours, agg_map, owners):
    elems = jacobian.shape[0]
    width = prolong.shape[1]
    aggs_here = owners.shape[0]
    rest = width - LANES
    size_x = lax.axis_size("gx")
    size_y = lax.axis_size("gy")
    size_z = lax.axis_size("gz")
    per_owner = aggs_here // 4
    out_slots = size_z * per_owner
    device = (lax.axis_index("gx") * size_y + lax.axis_index("gy")) * size_z + lax.axis_index("gz")
    nbr = neighbours.T
    local_ids = nbr - device * elems
    on_device = (local_ids >= 0) & (local_ids < elems)
    is_valid = nbr >= 0
    face_sizes = (LY * LZ, LX * LZ, LX * LY)
    ids = jnp.arange(elems, dtype=jnp.int32)
    agg_local = agg_map - device * aggs_here

    off_side = jnp.logical_not(on_device)
    before = ids[None, :] < ids[:, None]
    face_rank = jnp.sum((off_side[:, None, :] & before[None]).astype(jnp.int32), axis=2)
    ranks = jnp.arange(max(face_sizes), dtype=jnp.int32)
    chosen = off_side[:, None, :] & (face_rank[:, None, :] == ranks[None, :, None])
    by_side = jnp.sum(jnp.where(chosen, ids, 0), axis=2)

    off_valid = off_side & is_valid
    lower = off_valid[:, None, :] & (nbr[:, None, :] < nbr[:, :, None])
    position = jnp.sum(lower.astype(jnp.int32), axis=2)
    zero_xy = elems + max(face_sizes[:2])
    zero_z = elems + face_sizes[2]
    zeros = jnp.where(jnp.arange(6) < 4, zero_xy, zero_z)[:, None].astype(jnp.int32)
    column = jnp.where(on_device, local_ids, elems + position)
    column = jnp.where(is_valid, column, zeros)
    near_agg = jnp.sum(jnp.where(local_ids[:, :, None] == ids, agg_local, 0), axis=2)
    same_agg = on_device & (near_agg == agg_local[None, :])
    codes = column * 2 + same_agg.astype(jnp.int32)
    table = jnp.concatenate([ids[None] * 2 + 1, codes, agg_local[None]], axis=0)

    sends = [d ^ 1 for d in range(6)]
    if size_x == 2:
        swap = jnp.where(lax.axis_index("gx") == 0, by_side[1], by_side[0])
        picks = jnp.stack([by_side[5], by_side[4], by_side[3], by_side[2], swap])
        counts = [face_sizes[2]] * 2 + [face_sizes[1]] * 2 + [face_sizes[0]]
    else:
        picks = jnp.stack([by_side[sends[d]] for d in (4, 5, 2, 3, 0, 1)])
        counts = [face_sizes[d // 2] for d in (4, 5, 2, 3, 0, 1)]
    packed = pack_kernel(picks, prolong, counts)
    z_up = from_behind(packed[0], "gz", 1)
    z_down = from_behind(packed[1], "gz", -1)
    z_faces = [z_up, z_down]
    y_faces = [from_behind(packed[2], "gy", 1), from_behind(packed[3], "gy", -1)]
    if size_x == 2:
        x_faces = [lax.ppermute(packed[4], "gx", [(0, 1), (1, 0)])] * 2
    else:
        x_faces = [from_behind(packed[4], "gx", 1), from_behind(packed[5], "gx", -1)]

    agg_hot = (agg_local[:, None] == jnp.arange(aggs_here, dtype=jnp.int32)).astype(jnp.float32)
    per_element = jnp.einsum("eji,ej->ei", prolong, residual, preferred_element_type=jnp.float32)
    restr = jnp.dot(per_element.T, agg_hot, precision=lax.Precision.HIGHEST).astype(jnp.bfloat16)

    agg_counter = jnp.arange(aggs_here, dtype=jnp.int32)
    earlier = (owners[None, :] == owners[:, None]) & (agg_counter[None, :] < agg_counter[:, None])
    within = jnp.sum(earlier.astype(jnp.int32), axis=1)
    dest = owners * per_owner + within

    jac = jnp.transpose(jacobian, (1, 2, 0, 3))
    carry, flipped = own_kernel(table, prolong, jac, aggs_here)
    first, carry = side_kernel(
        table, dest, prolong, flipped, carry, x_faces + y_faces, jac, 1, out_slots
    )
    first = lax.all_to_all(first, "gz", split_axis=0, concat_axis=0, tiled=True)
    (second,) = side_kernel(
        table, dest, prolong, flipped, carry, z_faces, jac, 5, out_slots, restr=restr
    )
    second = lax.all_to_all(second, "gz", split_axis=0, concat_axis=0, tiled=True)

    def tails(part, rows):
        packed_tail = part[:, rows, :, : rows * rest]
        return packed_tail.reshape(-1, width, rows, rest).transpose(0, 2, 1, 3)

    first_tails, second_tails = tails(first, 4), tails(second, 3)
    heads = jnp.concatenate([second[:, :1], first[:, :4], second[:, 1:3]], axis=1)
    ends = jnp.concatenate([second_tails[:, :1], first_tails, second_tails[:, 1:]], axis=1)
    restricted = second[:, 3, :, 3 * rest]
    return (jnp.concatenate([heads, ends], axis=3), restricted)


def solution(mesh):
    return jax.shard_map(
        body,
        mesh=mesh,
        in_specs=(
            P(("gx", "gy", "gz"), None, None, None),
            P(("gx", "gy", "gz"), None, None),
            P(("gx", "gy", "gz"), None),
            P(("gx", "gy", "gz"), None),
            P(("gx", "gy", "gz")),
            P(("gx", "gy", "gz")),
        ),
        out_specs=(P(("gx", "gy", "gz"), None, None, None), P(("gx", "gy", "gz"), None)),
        check_vma=False,
    )
```

```python
import jax
import jax.numpy as jnp
from jax import lax
from jax.experimental import pallas as pl
from jax.experimental.pallas import tpu as pltpu
from jax.sharding import PartitionSpec as P


LX = 4
LY = 4
LZ = 2
LANES = 128
UNROLL = 16


def from_behind(value, axis, steps):
    count = lax.axis_size(axis)
    initial, last = (max(0, -steps), min(count, count - steps))
    return lax.ppermute(value, axis, [(source, source + steps) for source in range(initial, last)])


def whole():
    return pl.BlockSpec(memory_space=pltpu.VMEM)


def params():
    return pltpu.CompilerParams(vmem_limit_bytes=56 << 20)


def cost(pairs, width):
    return pl.CostEstimate(
        flops=pairs * 96 * width * width * width,
        bytes_accessed=pairs * 4 * width * width,
        transcendentals=0,
    )


def pack_kernel(picks, prolong, counts):
    _, width, _ = prolong.shape
    rest = width - LANES

    def kernel(pick_ref, p_ref, *outs):
        for d, (out, count) in enumerate(zip(outs, counts)):
            for n in range(count):
                block = p_ref[pick_ref[d, n]]
                out[n] = block[:, :LANES]
                out[count, :, n * rest : (n + 1) * rest] = block[:, LANES:]

    return pl.pallas_call(
        kernel,
        grid_spec=pltpu.PrefetchScalarGridSpec(
            num_scalar_prefetch=1,
            grid=(1,),
            in_specs=[whole()],
            out_specs=[whole()] * len(counts),
        ),
        out_shape=[jax.ShapeDtypeStruct((n + 1, width, LANES), prolong.dtype) for n in counts],
        compiler_params=params(),
    )(picks, prolong)


def pitch(elems):
    return elems + 1


def spread(j_ref, near, far):
    _, width, elems, _ = j_ref.shape
    step_rows = 5 if width % 5 == 0 else 1
    rest = width - LANES

    @pl.loop(0, width // step_rows)
    def _(c):
        part = j_ref[0, pl.ds(c * step_rows, step_rows)].astype(jnp.float32)
        for r in range(step_rows):
            rows = pl.ds((c * step_rows + r) * pitch(elems), elems)
            near[rows, :] = part[r, :, :LANES]
            far[rows, :rest] = part[r, :, LANES:]


def own_block(near, far, e, width, elems):
    rows = pl.ds(e, width, stride=pitch(elems))
    both = jnp.concatenate([near[rows, :], far[rows, :]], axis=1)
    return both[:, :width].astype(jnp.bfloat16)


def mul(a, b):
    return jnp.dot(a, b, preferred_element_type=jnp.float32)


def spread_scratch(width, elems):
    return [pltpu.VMEM((width * pitch(elems), LANES), jnp.float32)] * 2


def jac_spec(width, elems, first):
    return pl.BlockSpec((1, width, elems, width), lambda k, *_: (first + k, 0, 0, 0))


def own_kernel(table, prolong, jac, aggs_here):
    elems, width, _ = prolong.shape

    def kernel(table_ref, p_ref, j_ref, total, flipped, near, far):
        total[...] = jnp.zeros_like(total)
        spread(j_ref, near, far)

        @pl.loop(0, elems // UNROLL)
        def _(group):
            at = [group * UNROLL + u for u in range(UNROLL)]
            products = [
                mul(own_block(near, far, e, width, elems), p_ref[e]).astype(jnp.bfloat16)
                for e in at
            ]
            turned = [p_ref[e].astype(jnp.float32).T.astype(flipped.dtype) for e in at]
            triples = [mul(t, product) for t, product in zip(turned, products)]
            for e, t, triple in zip(at, turned, triples):
                flipped[e] = t
                total[table_ref[7, e]] += triple

    return pl.pallas_call(
        kernel,
        grid_spec=pltpu.PrefetchScalarGridSpec(
            num_scalar_prefetch=1,
            grid=(1,),
            in_specs=[whole(), jac_spec(width, elems, 0)],
            out_specs=[whole(), whole()],
            scratch_shapes=spread_scratch(width, elems),
        ),
        out_shape=[
            jax.ShapeDtypeStruct((aggs_here, width, width), jnp.float32),
            jax.ShapeDtypeStruct(prolong.shape, prolong.dtype),
        ],
        cost_estimate=cost(elems, width),
        compiler_params=params(),
    )(table, prolong, jac)


def side_kernel(table, dest, prolong, flipped, carry, faces, jac, first, out_slots, restr=None):
    elems, width, _ = prolong.shape
    aggs_here = carry.shape[0]
    rest = width - LANES
    count = len(faces)
    zero_block = elems + max(face.shape[0] for face in faces) - 1
    final = restr is not None
    emitted = range(0 if final else 1, count + 1)
    rows_out = len(emitted)
    tall = pl.cdiv(width, 8) * 8

    def kernel(table_ref, dest_ref, p_ref, t_ref, carry_ref, *refs):
        face_refs, refs = refs[:count], refs[count:]
        if final:
            restr_ref, refs = refs[0], refs[1:]
        j_ref, out, refs = refs[0], refs[1], refs[2:]
        if not final:
            next_ref, refs = refs[0], refs[1:]
        pool, near, far, total = refs
        k = pl.program_id(0)

        @pl.when(k == 0)
        def _():
            out[...] = jnp.zeros_like(out)
            total[...] = jnp.zeros_like(total)
            pool[zero_block] = jnp.zeros((width, width), pool.dtype)

            @pl.loop(0, aggs_here)
            def _(a):
                total[a, 0] = carry_ref[a]

            @pl.loop(0, elems)
            def _(e):
                pool[e] = p_ref[e]

        for d, face_ref in enumerate(face_refs):

            @pl.when(k == d)
            def _(face_ref=face_ref):
                last = face_ref.shape[0] - 1
                for n in range(last):
                    pool[elems + n, :, :LANES] = face_ref[n]
                    pool[elems + n, :, LANES:] = face_ref[last, :, n * rest : (n + 1) * rest]

        spread(j_ref, near, far)

        @pl.loop(0, elems // UNROLL)
        def _(group):
            at = [group * UNROLL + u for u in range(UNROLL)]
            codes = [table_ref[first + k, e] for e in at]
            products = [
                mul(own_block(near, far, e, width, elems), pool[code // 2]).astype(jnp.bfloat16)
                for e, code in zip(at, codes)
            ]
            triples = [mul(t_ref[e], product) for e, product in zip(at, products)]
            for e, code, triple in zip(at, codes, triples):
                total[table_ref[7, e], jnp.where(code % 2 == 1, 0, k + 1)] += triple

        @pl.when(k == count - 1)
        def _():
            for a in range(aggs_here):
                to = dest_ref[a]
                for i, s in enumerate(emitted):
                    row = total[a, s].astype(jnp.bfloat16)
                    out[to, i * tall : i * tall + width, :] = row[:, :LANES]
                    lanes = slice(i * rest, (i + 1) * rest)
                    out[to, rows_out * tall : rows_out * tall + width, lanes] = row[:, LANES:]
                if final:
                    below = (rows_out + 1) * tall
                    out[to, below : below + 1, :] = restr_ref[a : a + 1, :LANES]
                    out[to, below + 1 : below + 2, :rest] = restr_ref[a : a + 1, LANES:]
                else:
                    next_ref[a] = total[a, 0]

    rows_all = (rows_out + 1) * tall + (8 if final else 0)
    out_shape = [jax.ShapeDtypeStruct((out_slots, rows_all, LANES), jnp.bfloat16)]
    if not final:
        out_shape.append(jax.ShapeDtypeStruct(carry.shape, carry.dtype))
    inputs = [prolong, flipped, carry, *faces] + ([restr] if final else [])
    return pl.pallas_call(
        kernel,
        grid_spec=pltpu.PrefetchScalarGridSpec(
            num_scalar_prefetch=2,
            grid=(count,),
            in_specs=[whole()] * len(inputs) + [jac_spec(width, elems, first)],
            out_specs=[whole()] * len(out_shape),
            scratch_shapes=[pltpu.VMEM((zero_block + 1, width, width), jnp.bfloat16)]
            + spread_scratch(width, elems)
            + [pltpu.VMEM((aggs_here, count + 1, width, width), jnp.float32)],
        ),
        out_shape=out_shape,
        cost_estimate=cost(elems * count, width),
        compiler_params=params(),
    )(table, dest, *inputs, jac)


def body(jacobian, prolong, residual, neighbours, agg_map, owners):
    elems = jacobian.shape[0]
    width = prolong.shape[1]
    aggs_here = owners.shape[0]
    rest = width - LANES
    size_x = lax.axis_size("gx")
    size_y = lax.axis_size("gy")
    size_z = lax.axis_size("gz")
    per_owner = aggs_here // 4
    out_slots = size_z * per_owner
    device = (lax.axis_index("gx") * size_y + lax.axis_index("gy")) * size_z + lax.axis_index("gz")
    nbr = neighbours.T
    local_ids = nbr - device * elems
    on_device = (local_ids >= 0) & (local_ids < elems)
    is_valid = nbr >= 0
    face_sizes = (LY * LZ, LX * LZ, LX * LY)
    ids = jnp.arange(elems, dtype=jnp.int32)
    agg_local = agg_map - device * aggs_here

    off_side = jnp.logical_not(on_device)
    before = ids[None, :] < ids[:, None]
    face_rank = jnp.sum((off_side[:, None, :] & before[None]).astype(jnp.int32), axis=2)
    ranks = jnp.arange(max(face_sizes), dtype=jnp.int32)
    chosen = off_side[:, None, :] & (face_rank[:, None, :] == ranks[None, :, None])
    by_side = jnp.sum(jnp.where(chosen, ids, 0), axis=2)

    off_valid = off_side & is_valid
    lower = off_valid[:, None, :] & (nbr[:, None, :] < nbr[:, :, None])
    position = jnp.sum(lower.astype(jnp.int32), axis=2)
    zero_xy = elems + max(face_sizes[:2])
    zero_z = elems + face_sizes[2]
    zeros = jnp.where(jnp.arange(6) < 4, zero_xy, zero_z)[:, None].astype(jnp.int32)
    column = jnp.where(on_device, local_ids, elems + position)
    column = jnp.where(is_valid, column, zeros)
    near_agg = jnp.sum(jnp.where(local_ids[:, :, None] == ids, agg_local, 0), axis=2)
    same_agg = on_device & (near_agg == agg_local[None, :])
    codes = column * 2 + same_agg.astype(jnp.int32)
    table = jnp.concatenate([ids[None] * 2 + 1, codes, agg_local[None]], axis=0)

    sends = [d ^ 1 for d in range(6)]
    if size_x == 2:
        swap = jnp.where(lax.axis_index("gx") == 0, by_side[1], by_side[0])
        picks = jnp.stack([by_side[5], by_side[4], by_side[3], by_side[2], swap])
        counts = [face_sizes[2]] * 2 + [face_sizes[1]] * 2 + [face_sizes[0]]
    else:
        picks = jnp.stack([by_side[sends[d]] for d in (4, 5, 2, 3, 0, 1)])
        counts = [face_sizes[d // 2] for d in (4, 5, 2, 3, 0, 1)]
    packed = pack_kernel(picks, prolong, counts)
    z_up = from_behind(packed[0], "gz", 1)
    z_down = from_behind(packed[1], "gz", -1)
    z_faces = [z_up, z_down]
    y_faces = [from_behind(packed[2], "gy", 1), from_behind(packed[3], "gy", -1)]
    if size_x == 2:
        x_faces = [lax.ppermute(packed[4], "gx", [(0, 1), (1, 0)])] * 2
    else:
        x_faces = [from_behind(packed[4], "gx", 1), from_behind(packed[5], "gx", -1)]

    agg_hot = (agg_local[:, None] == jnp.arange(aggs_here, dtype=jnp.int32)).astype(jnp.float32)
    per_element = jnp.einsum("eji,ej->ei", prolong, residual, preferred_element_type=jnp.float32)
    restr = jnp.dot(agg_hot.T, per_element, precision=lax.Precision.HIGHEST).astype(jnp.bfloat16)

    agg_counter = jnp.arange(aggs_here, dtype=jnp.int32)
    earlier = (owners[None, :] == owners[:, None]) & (agg_counter[None, :] < agg_counter[:, None])
    within = jnp.sum(earlier.astype(jnp.int32), axis=1)
    dest = owners * per_owner + within

    jac = jnp.transpose(jacobian, (1, 2, 0, 3))
    carry, flipped = own_kernel(table, prolong, jac, aggs_here)
    first, carry = side_kernel(
        table, dest, prolong, flipped, carry, x_faces + y_faces, jac, 1, out_slots
    )
    first = lax.all_to_all(first, "gz", split_axis=0, concat_axis=0, tiled=True)
    (second,) = side_kernel(
        table, dest, prolong, flipped, carry, z_faces, jac, 5, out_slots, restr=restr
    )
    second = lax.all_to_all(second, "gz", split_axis=0, concat_axis=0, tiled=True)

    tall = pl.cdiv(width, 8) * 8

    def split(part, rows):
        blocks = part[:, : (rows + 1) * tall].reshape(-1, rows + 1, tall, LANES)[:, :, :width]
        packed_tail = blocks[:, rows, :, : rows * rest]
        return blocks, packed_tail.reshape(-1, width, rows, rest).transpose(0, 2, 1, 3)

    first_heads, first_tails = split(first, 4)
    second_heads, second_tails = split(second, 3)
    heads = jnp.concatenate([second_heads[:, :1], first_heads[:, :4], second_heads[:, 1:3]], axis=1)
    ends = jnp.concatenate([second_tails[:, :1], first_tails, second_tails[:, 1:]], axis=1)
    below = second[:, 4 * tall : 4 * tall + 2, :]
    restricted = jnp.concatenate([below[:, 0, :], below[:, 1, :rest]], axis=1)
    return (jnp.concatenate([heads, ends], axis=3), restricted)


def solution(mesh):
    return jax.shard_map(
        body,
        mesh=mesh,
        in_specs=(
            P(("gx", "gy", "gz"), None, None, None),
            P(("gx", "gy", "gz"), None, None),
            P(("gx", "gy", "gz"), None),
            P(("gx", "gy", "gz"), None),
            P(("gx", "gy", "gz")),
            P(("gx", "gy", "gz")),
        ),
        out_specs=(P(("gx", "gy", "gz"), None, None, None), P(("gx", "gy", "gz"), None)),
        check_vma=False,
    )
```
